256 devices in a mesh: ctx: 32 (over x, z), head: 8 (over y, core).
Axes of the slice: x: 4, y: 4, z: 8, core: 2. Of those that a mesh axis runs over, the one named last changes fastest.
Arguments:
- queries: bfloat16 [32768, 5120], P('ctx', 'head'), may hold values from -60 to 60
- key_rows: bfloat16 [32768, 5120], P('ctx', 'head'), may hold values from -10 to 10
- value_rows: bfloat16 [32768, 5120], P('ctx', 'head'), may hold values from -60 to 60
- norm_gain: float32 [5120], P('head'), may hold values from 0.1 to 1.9
- sort_index: int32 [128], replicated, may hold values from 0 to 127
- grad_normed: bfloat16 [32768, 5120], P('ctx', 'head'), may hold values from -6 to 6
Outputs:
- normed: bfloat16 [32768, 5120], P('ctx', 'head')
- grad_queries: bfloat16 [32768, 5120], P('ctx', 'head')
- grad_keys: bfloat16 [32768, 5120], P('ctx', 'head')
- grad_values: bfloat16 [32768, 5120], P('ctx', 'head')
The draws below stay inside these ranges and needn't reach their ends.
Inputs may be any that keep to these rules, and one draw needn't show every extreme that they name: `sort_index`: several query blocks may name the same block.
All inputs are finite; a program needn't handle non-finite values.
Results may differ from the reference program's by a relative error of at most 0.009.
Values may be sent and summed in bfloat16 or wider, within the bound.
A program may use at most 128 MiB of HBM per device.

```python
import math
import jax
import jax.numpy as jnp
import numpy as np
from jax import lax

HEADS = 40
HDIM = 128
BLOCK = 256
NBLK = 128
SEQ = 32768
WIDTH = 5120


def drawn_parts(key):
    base = jax.random.normal(jax.random.fold_in(key, 11), (SEQ, WIDTH), jnp.float32)
    return base


def draw_queries(key, part):
    private = jnp.clip(jax.random.normal(jax.random.fold_in(key, 14), (SEQ, WIDTH), jnp.float32), -6.0, 6.0)
    return private.astype(jnp.bfloat16)


def draw_key_rows(key, part):
    base = drawn_parts(key)
    drawn = jnp.clip(base, -6.0, 6.0)
    return drawn.astype(jnp.bfloat16)


def draw_value_rows(key, part):
    column = jnp.arange(WIDTH)[None, :] // HDIM
    share = column.astype(jnp.float32) / max(HEADS - 1, 1)
    level = jax.random.uniform(jax.random.fold_in(key, 22), (SEQ, 1), jnp.float32)
    noise = jax.random.normal(jax.random.fold_in(key, 21), (SEQ, WIDTH), jnp.float32)
    factor = 10.0 ** (0.5 * share) * 10.0 ** (0.5 * level)
    return jnp.clip(noise * factor, -60.0, 60.0).astype(jnp.bfloat16)


def touch_ends(array, stream_key, smallest, high):
    longest = array.shape.index(max(array.shape))
    spots = []
    for shift in (0, 1):
        where = [jax.random.randint(jax.random.fold_in(stream_key, axis), (), 0, length) for axis, length in enumerate(array.shape)]
        where[longest] = (where[longest] + shift) % array.shape[longest]
        spots.append(tuple(where))
    return array.at[spots[0]].set(smallest).at[spots[1]].set(high)


def block_levels(own_key, dims, pieces, low, largest):
    def one(dim, shards_of):
        heights = jax.random.uniform(jax.random.fold_in(jax.random.fold_in(own_key, 6), dim), (shards_of,), jnp.float32, low / len(pieces), largest / len(pieces))
        return jnp.repeat(jnp.exp(heights), dims[dim] // shards_of).reshape((-1,) + (1,) * (len(dims) - dim - 1))

    factor_of = one(*pieces[0])
    for cut in pieces[1:]:
        factor_of = factor_of * one(*cut)
    return factor_of


def cumulative_ranks(number_of, slope):
    weights = [(1 << 20) // math.isqrt(rank ** slope) + 1 for rank in range(1, number_of + 1)]
    deviation = 1 + sum(weights) // (1 << 30)
    return np.cumsum(np.array([max(1, weight // deviation) for weight in weights]))


def ranked_ids(stream_key, shape, count, slope):
    listing = cumulative_ranks(count, slope)
    lot = jax.random.randint(jax.random.fold_in(stream_key, 1), shape, 0, int(listing[count - 1]))
    rank = jnp.searchsorted(jnp.asarray(listing, jnp.int32), lot, side="right")
    return jax.random.permutation(jax.random.fold_in(stream_key, 2), count)[rank].astype(jnp.int32)


def scatter_about(rng, extent, deviation, reach, shards=(), kind=jnp.bfloat16):
    level = block_levels(rng, extent, shards, -0.22, 0.18) if shards else 1.0
    values = jax.random.normal(rng, extent, jnp.float32) * deviation * level
    return jnp.minimum(jnp.maximum(values, -reach), reach).astype(kind)


def setup_inputs(seed: int = 0) -> dict:
    streams_of = jax.random.split(jax.random.key(seed), 7)
    queries = draw_queries(jax.random.fold_in(streams_of[6], 71), 0)
    key_rows = draw_key_rows(jax.random.fold_in(streams_of[6], 71), 0)
    value_rows = draw_value_rows(jax.random.fold_in(streams_of[6], 71), 0)
    norm_gain = jnp.clip(1.0 + 0.18 * jax.random.normal(streams_of[3], (WIDTH,), jnp.float32), 0.1, 1.9)
    sort_index = touch_ends(ranked_ids(streams_of[4], (NBLK,), NBLK, 2), jax.random.fold_in(streams_of[4], 3), 0, NBLK - 1).astype(jnp.int32)
    grad_normed = scatter_about(streams_of[5], (SEQ, WIDTH), 1.0, 6.0, ((0, 32), (1, 8)))
    return dict(queries=queries, key_rows=key_rows, value_rows=value_rows, norm_gain=norm_gain, sort_index=sort_index, grad_normed=grad_normed)


def allowed_keys(block_id):
    query_pos = jnp.arange(BLOCK)[:, None]
    key_pos = jnp.arange(BLOCK)[None, :]
    causal = key_pos <= query_pos
    before = jnp.broadcast_to(block_id > 0, (BLOCK, BLOCK))
    chosen = jnp.ones((BLOCK, BLOCK), dtype=jnp.bool_)
    return jnp.concatenate([causal, before, chosen], axis=1)

def probabilities(query_block, key_set, allowed):
    head_count = query_block.shape[1] // HDIM
    q_split = query_block.reshape(BLOCK, head_count, HDIM).astype(jnp.float32)
    k_split = key_set.reshape(3 * BLOCK, head_count, HDIM).astype(jnp.float32)
    scores = jnp.einsum('qhd,khd->hqk', q_split, k_split) * HDIM ** (-0.5)
    scores = jnp.where(allowed[None], scores, -jnp.inf)
    highest = lax.optimization_barrier(jnp.max(scores, axis=2, keepdims=True))
    weights = jnp.exp(scores - highest)
    return weights / lax.optimization_barrier(jnp.sum(weights, axis=2, keepdims=True))

def reference(queries, key_rows, value_rows, norm_gain, sort_index, grad_normed):
    q_blocks = queries.reshape(NBLK, BLOCK, WIDTH)
    k_blocks = key_rows.reshape(NBLK, BLOCK, WIDTH)
    v_blocks = value_rows.reshape(NBLK, BLOCK, WIDTH)
    block_ids = jnp.arange(NBLK, dtype=jnp.int32)
    before_ids = jnp.maximum(block_ids - 1, 0).astype(jnp.int32)

    def gather_set(blocks, index):
        return jnp.concatenate([blocks[index], blocks[before_ids[index]], blocks[sort_index[index]]], axis=0)

    def forward(index):
        key_set = gather_set(k_blocks, index)
        value_set = gather_set(v_blocks, index)
        probs = probabilities(q_blocks[index], key_set, allowed_keys(index))
        probs_low = probs.astype(jnp.bfloat16).astype(jnp.float32)
        v_split = value_set.reshape(3 * BLOCK, HEADS, HDIM).astype(jnp.float32)
        result = jnp.einsum('hqk,khd->qhd', probs_low, v_split)
        return result.reshape(BLOCK, WIDTH)
    attended = lax.map(forward, block_ids).reshape(SEQ, WIDTH)
    inv_rms = lax.rsqrt(lax.optimization_barrier(jnp.mean(attended * attended, axis=1, keepdims=True)) + 1e-05)
    normed = (attended * inv_rms * norm_gain).astype(jnp.bfloat16)
    lifted = norm_gain * grad_normed.astype(jnp.float32)
    center = lax.optimization_barrier(jnp.sum(lifted * attended, axis=1, keepdims=True))
    grad_attended = (inv_rms * lifted - attended * inv_rms ** 3 * center / WIDTH).astype(jnp.bfloat16)
    g_blocks = grad_attended.reshape(NBLK, BLOCK, WIDTH)

    def backward(index):
        key_set = gather_set(k_blocks, index)
        value_set = gather_set(v_blocks, index)
        probs = probabilities(q_blocks[index], key_set, allowed_keys(index))
        probs_low = probs.astype(jnp.bfloat16).astype(jnp.float32)
        q_split = q_blocks[index].reshape(BLOCK, HEADS, HDIM).astype(jnp.float32)
        k_split = key_set.reshape(3 * BLOCK, HEADS, HDIM).astype(jnp.float32)
        v_split = value_set.reshape(3 * BLOCK, HEADS, HDIM).astype(jnp.float32)
        d_split = g_blocks[index].reshape(BLOCK, HEADS, HDIM).astype(jnp.float32)
        grad_set_v = jnp.einsum('hqk,qhd->khd', probs_low, d_split).reshape(3 * BLOCK, WIDTH)
        grad_probs = jnp.einsum('qhd,khd->hqk', d_split, v_split)
        row_center = lax.optimization_barrier(jnp.sum(probs * grad_probs, axis=2, keepdims=True))
        grad_scores = (probs * (grad_probs - row_center) * HDIM ** (-0.5)).astype(jnp.bfloat16).astype(jnp.float32)
        grad_q = jnp.einsum('hqk,khd->qhd', grad_scores, k_split).reshape(BLOCK, WIDTH).astype(jnp.bfloat16)
        grad_set_k = jnp.einsum('hqk,qhd->khd', grad_scores, q_split).reshape(3 * BLOCK, WIDTH)
        return (grad_q, grad_set_k[:BLOCK], grad_set_k[BLOCK:].astype(jnp.bfloat16), grad_set_v[:BLOCK], grad_set_v[BLOCK:].astype(jnp.bfloat16))
    grad_q, own_k, far_k, own_v, far_v = lax.map(backward, block_ids)

    def settle(own_part, far_part):
        before_part = far_part[:, :BLOCK].astype(jnp.float32)
        chosen_part = far_part[:, BLOCK:].astype(jnp.float32)
        shifted = jnp.concatenate([before_part[1:], jnp.zeros_like(before_part[:1])], axis=0)
        summed = jax.ops.segment_sum(chosen_part, sort_index, num_segments=NBLK)
        return (own_part + shifted + summed).astype(jnp.bfloat16).reshape(SEQ, WIDTH)
    grad_keys = settle(own_k, far_k)
    grad_values = settle(own_v, far_v)
    return (normed, grad_q.reshape(SEQ, WIDTH), grad_keys, grad_values)
```

```python
import functools

import jax
import jax.numpy as jnp
from jax import lax
from jax.experimental import pallas as pl
from jax.experimental.pallas import tpu as pltpu
from jax.sharding import PartitionSpec as P

HDIM = 128
BLOCK = 256
WIDTH = 5120
EPS = 1e-05
SCALE = HDIM**-0.5
LOG2E = 1.4426950408889634
MESH = pl.DeviceIdType.MESH

CTX = 32
XS, ZS = 4, 8
PEERS = 8
NB = 4
NBLK = CTX * NB
ROWS = BLOCK // CTX
HEADS = 5
COLS = HEADS * HDIM

NT = (((1,), (1,)), ((), ()))
NN = (((1,), (0,)), ((), ()))
TN = (((0,), (0,)), ((), ()))

P1K, P1V, P2K, P2V, B1K, B1V, B2K, B2V, BEK, BEV, GBK, GBV, STA = 0, 1, 2, 6, 10, 11, 12, 13, 14, 15, 16, 17, 18
NSEM = 22


def dot(a, b, dims):
    return lax.dot_general(a, b, dims, preferred_element_type=jnp.float32)


def share(t):
    return pl.ds(pl.multiple_of(t * ROWS, ROWS), ROWS)


def kernel(
    idx, gain, q_hbm, k_hbm, v_hbm, g_hbm,
    n_out, dq_out, dk_out, dv_out,
    qv, kx, vx, gv, sk, sv, pk, pv, rk, rv, pst, att, sq, sc, st, hs, ga,
    dks, dvs, kacc, vacc, kbs, vbs, kbr, vbr, tk, tv, hk, hv, tgt, nv, dqv,
    ssem, rsem, lsem, osem,
):
    cx = lax.axis_index("ctx")
    hd = lax.axis_index("head")
    x, z = cx // ZS, lax.rem(cx, ZS)

    def peer(d):
        return lax.rem(x + d // ZS, XS) * ZS + lax.rem(z + lax.rem(d, ZS), ZS)

    nxt = lax.rem(cx + 1, CTX)
    prv = lax.rem(cx + CTX - 1, CTX)

    loads = [
        pltpu.make_async_copy(q_hbm, qv, lsem.at[0]),
        pltpu.make_async_copy(k_hbm, kx.at[pl.ds(1, NB)], lsem.at[1]),
        pltpu.make_async_copy(v_hbm, vx.at[pl.ds(1, NB)], lsem.at[2]),
        pltpu.make_async_copy(g_hbm, gv, lsem.at[3]),
    ]
    for c in loads:
        c.start()

    bar = pltpu.get_barrier_semaphore()

    def greet_ctx(d, _):
        pl.semaphore_signal(bar, 1, device_id=(peer(d), hd), device_id_type=MESH)
        return 0

    def greet_head(d, _):
        pl.semaphore_signal(bar, 1, device_id=(cx, lax.rem(hd + d, PEERS)), device_id_type=MESH)
        return 0

    lax.fori_loop(1, CTX, greet_ctx, 0)
    lax.fori_loop(1, PEERS, greet_head, 0)
    pl.semaphore_wait(bar, CTX - 1 + PEERS - 1)

    def remote(src, dst, send, recv, target):
        pltpu.make_async_remote_copy(
            src, dst, ssem.at[send], rsem.at[recv], device_id=target, device_id_type=MESH
        ).start()

    def spread(src_of, dst, send, recv):
        def one(d, _):
            t = peer(d)
            remote(src_of(t), dst, send, recv, (t, hd))
            return 0

        lax.fori_loop(1, CTX, one, 0)
        pltpu.make_async_copy(src_of(cx), dst, rsem.at[recv]).start()

    def arrived(ref, s):
        pltpu.make_async_copy(ref, ref, rsem.at[s]).wait()

    def sent(ref, s):
        pltpu.make_async_copy(ref, ref, ssem.at[s]).wait()

    own4 = pl.ds(cx * NB, NB)

    spread(lambda t: k_hbm.at[:, share(t), :], sk.at[own4], P1K, P1K)
    spread(lambda t: v_hbm.at[:, share(t), :], sv.at[own4], P1V, P1V)
    remote(k_hbm.at[NB - 1], kx.at[0], BEK, BEK, (nxt, hd))
    remote(v_hbm.at[NB - 1], vx.at[0], BEV, BEV, (nxt, hd))

    lane = lax.broadcasted_iota(jnp.int32, (1, NBLK * ROWS), 1)

    def fill(i, t):
        return jnp.where(lane // ROWS == i, idx[i], t)

    tgt[...] = lax.fori_loop(0, NBLK, fill, jnp.zeros_like(lane)) * ROWS + lax.rem(lane, ROWS)

    def select(s, p):
        def one(i, _):
            p[i] = s[idx[i]]
            return 0

        lax.fori_loop(0, NBLK, one, 0)

    def phase2(p, r, base):
        def block(b, _):
            spread(lambda t: p.at[t * NB + b], r.at[b, share(cx)], base, base + b)
            return 0

        lax.fori_loop(0, NB, block, 0)

    arrived(sk, P1K)
    select(sk, pk)
    phase2(pk, rk, P2K)
    arrived(sv, P1V)
    select(sv, pv)
    phase2(pv, rv, P2V)
    for c in loads:
        c.wait()
    arrived(kx.at[0], BEK)
    arrived(vx.at[0], BEV)

    causal = lax.broadcasted_iota(jnp.int32, (BLOCK, BLOCK), 0) <= lax.broadcasted_iota(
        jnp.int32, (BLOCK, BLOCK), 1
    )

    def head_cols(h):
        return pl.ds(pl.multiple_of(h * HDIM, HDIM), HDIM)

    def forward(b):
        par = lax.rem(b, 2)
        arrived(rk.at[b], P2K + b)
        arrived(rv.at[b], P2V + b)
        sq[...] = jnp.zeros_like(sq)
        sc[...] = jnp.zeros_like(sc)
        follows = cx * NB + b > 0

        def head(h, _):
            cols = head_cols(h)
            q = qv[b, :, cols]
            s0 = jnp.where(causal, dot(kx[b + 1, :, cols], q, NT), -jnp.inf)
            s1 = jnp.where(follows, dot(kx[b, :, cols], q, NT), -jnp.inf)
            s2 = dot(rk[b, :, cols], q, NT)
            m = jnp.max(jnp.maximum(jnp.maximum(s0, s1), s2), axis=0, keepdims=True)
            e = [jnp.exp2((s - m) * (SCALE * LOG2E)) for s in (s0, s1, s2)]
            r = 1.0 / jnp.sum(e[0] + e[1] + e[2], axis=0, keepdims=True)
            p = [(w * r).astype(jnp.bfloat16) for w in e]
            for n in range(3):
                pst[par, h, n] = p[n]
            o = (
                dot(p[0], vx[b + 1, :, cols], TN)
                + dot(p[1], vx[b, :, cols], TN)
                + dot(p[2], rv[b, :, cols], TN)
            )
            att[par, :, cols] = o
            lifted = gain[:, cols] * gv[b, :, cols].astype(jnp.float32)
            sq[...] += o * o
            sc[...] += lifted * o
            return 0

        lax.fori_loop(0, HEADS, head, 0)
        st[b] = jnp.zeros((8, BLOCK), jnp.float32)
        st[b, 0:1, :] = jnp.sum(jnp.transpose(sq[...]), axis=0, keepdims=True)
        st[b, 1:2, :] = jnp.sum(jnp.transpose(sc[...]), axis=0, keepdims=True)

        def one(d, _):
            remote(st.at[b], hs.at[b, hd], STA + b, STA + b, (cx, lax.rem(hd + d, PEERS)))
            return 0

        lax.fori_loop(1, PEERS, one, 0)
        pltpu.make_async_copy(st.at[b], hs.at[b, hd], rsem.at[STA + b]).start()

    def backward(b):
        par = lax.rem(b, 2)
        arrived(hs.at[b], STA + b)
        total = jnp.sum(hs[b], axis=0)
        inv_row = lax.rsqrt(total[0:1, :] / WIDTH + EPS)
        cen_row = inv_row * inv_row * inv_row * total[1:2, :] / WIDTH
        inv = jnp.transpose(jnp.broadcast_to(inv_row, (HDIM, BLOCK)))
        cen = jnp.transpose(jnp.broadcast_to(cen_row, (HDIM, BLOCK)))

        def norm(h, _):
            cols = head_cols(h)
            a = att[par, :, cols]
            w = gain[:, cols]
            nv[b, :, cols] = (a * inv * w).astype(jnp.bfloat16)
            lifted = w * gv[b, :, cols].astype(jnp.float32)
            ga[:, cols] = (inv * lifted - a * cen).astype(jnp.bfloat16)
            return 0

        lax.fori_loop(0, HEADS, norm, 0)
        pltpu.make_async_copy(nv.at[b], n_out.at[b], osem.at[0]).start()

        def head(h, _):
            cols = head_cols(h)
            q = qv[b, :, cols]
            d = ga[:, cols]
            ks = (kx[b + 1, :, cols], kx[b, :, cols], rk[b, :, cols])
            vs = (vx[b + 1, :, cols], vx[b, :, cols], rv[b, :, cols])
            ps = [pst[par, h, n] for n in range(3)]
            dv = [dot(p, d, NN) for p in ps]
            dp = [dot(v, d, NT) for v in vs]
            pf = [p.astype(jnp.float32) for p in ps]
            row = jnp.sum(pf[0] * dp[0] + pf[1] * dp[1] + pf[2] * dp[2], axis=0, keepdims=True)
            ds = [(pf[n] * ((dp[n] - row) * SCALE)).astype(jnp.bfloat16) for n in range(3)]
            dk = [dot(s, q, NN) for s in ds]
            dq = dot(ds[0], ks[0], TN) + dot(ds[1], ks[1], TN) + dot(ds[2], ks[2], TN)
            dqv[b, :, cols] = dq.astype(jnp.bfloat16)
            vacc[b + 1, :, cols] = dv[0]
            kacc[b + 1, :, cols] = dk[0]
            kbe, vbe = dk[1].astype(jnp.bfloat16), dv[1].astype(jnp.bfloat16)

            @pl.when(b == 0)
            def _():
                kbs[:, cols] = kbe
                vbs[:, cols] = vbe

            @pl.when(b > 0)
            def _():
                kacc[b, :, cols] += kbe.astype(jnp.float32)
                vacc[b, :, cols] += vbe.astype(jnp.float32)

            dvs[b, :, cols] = dv[2].astype(jnp.bfloat16)
            dks[b, :, cols] = dk[2].astype(jnp.bfloat16)
            return 0

        lax.fori_loop(0, HEADS, head, 0)
        spread(lambda t: dvs.at[b, share(t)], tv.at[cx * NB + b], B1V, B1V)
        spread(lambda t: dks.at[b, share(t)], tk.at[cx * NB + b], B1K, B1K)
        pltpu.make_async_copy(dqv.at[b], dq_out.at[b], osem.at[1]).start()

        @pl.when(b == 0)
        def _():
            remote(kbs, kbr, GBK, GBK, (prv, hd))
            remote(vbs, vbr, GBV, GBV, (prv, hd))

    def step(s, _):
        @pl.when(s < NB)
        def _():
            forward(s)

        @pl.when(s > 0)
        def _():
            backward(s - 1)

        return 0

    lax.fori_loop(0, NB + 1, step, 0)

    chunk = 256

    def total(t, p):
        terms = t[...].reshape(NBLK * ROWS, COLS)

        def one(c, _):
            row = lax.broadcasted_iota(jnp.int32, (chunk, NBLK * ROWS), 0) + c * chunk
            table = jnp.where(row == tgt[...], 1.0, 0.0).astype(jnp.bfloat16)
            s = dot(table, terms, NN)
            p[pl.ds(c * (chunk // ROWS), chunk // ROWS)] = s.reshape(
                chunk // ROWS, ROWS, COLS
            ).astype(jnp.bfloat16)
            return 0

        lax.fori_loop(0, NBLK * ROWS // chunk, one, 0)

    most = pl.ds(0, NBLK - NB)
    sent(sv.at[most], P2V)
    arrived(tv, B1V)
    total(tv, pv)
    spread(lambda t: pv.at[pl.ds(t * NB, NB)], hv.at[:, share(cx), :], B2V, B2V)
    sent(sk.at[most], P2K)
    arrived(tk, B1K)
    total(tk, pk)
    spread(lambda t: pk.at[pl.ds(t * NB, NB)], hk.at[:, share(cx), :], B2K, B2K)
    arrived(kbr, GBK)
    arrived(vbr, GBV)

    def last(b, acc, h, edge, out):
        def head(j, _):
            cols = head_cols(j)
            out[b, :, cols] = (
                acc[b + 1, :, cols] + h[b, :, cols].astype(jnp.float32)
            ).astype(jnp.bfloat16)
            return 0

        return head

    def finish(acc, h, edge, out, dst, sem):
        def add(j, _):
            cols = head_cols(j)
            acc[NB, :, cols] += edge[:, cols].astype(jnp.float32)
            return 0

        lax.fori_loop(0, HEADS, add, 0)

        def block(b, _):
            lax.fori_loop(0, HEADS, last(b, acc, h, edge, out), 0)
            pltpu.make_async_copy(out.at[b], dst.at[b], osem.at[sem]).start()
            return 0

        lax.fori_loop(0, NB, block, 0)

    sent(dvs.at[:, pl.ds(0, BLOCK - ROWS), :], B1V)
    arrived(hv, B2V)
    finish(vacc, hv, vbr, dvs, dv_out, 2)
    sent(dks.at[:, pl.ds(0, BLOCK - ROWS), :], B1K)
    arrived(hk, B2K)
    finish(kacc, hk, kbr, dks, dk_out, 3)

    for s in (P1K, P1V, B2V, B2K):
        sent(sk.at[most], s)
    sent(kbs, BEK)
    sent(vbs, BEV)
    sent(kbs, GBK)
    sent(vbs, GBV)
    for b in range(NB):
        sent(hs.at[b, pl.ds(0, PEERS - 1)], STA + b)
    for s, (buf, dst) in enumerate(((nv, n_out), (dqv, dq_out), (dvs, dv_out), (dks, dk_out))):
        pltpu.make_async_copy(buf, dst, osem.at[s]).wait()


ROUNDS = 16
LEVELS = (16,)
LAG = 2
PLANE = XS * NB
QROWS = BLOCK // XS
CHUNKS = ((0, 3), (3, 2))
T_BLOCK, T_ROUND, T_SLOT, T_PICK, T_LAST, T_NEED = 0, 2, 4, 6, 7, 8


def router(idx, tab):
    row = lax.broadcasted_iota(jnp.int32, (ZS, NBLK), 0)
    lane = lax.broadcasted_iota(jnp.int32, (ZS, NBLK), 1)
    source = lax.rem(lane // NB, ZS)
    own = lane // (NB * ZS) * NB + lax.rem(lane, NB)
    rel = lax.rem(row - source + ZS, ZS)
    back = lax.rem(source - row + ZS, ZS)

    def ask(i, last):
        here = (row == lax.rem(i // NB, ZS)) & (lane == idx[i])
        return jnp.where(here, i // (NB * ZS) * NB + lax.rem(i, NB), last)

    last = lax.fori_loop(0, NBLK, ask, jnp.full((ZS, NBLK), PLANE, jnp.int32), unroll=8)
    asked = last < PLANE

    best = plus = minus = None
    for a in range(ZS):
        p = jnp.max(jnp.where(asked & (rel <= a), rel, 0), axis=0, keepdims=True)
        m = jnp.max(jnp.where(asked & (rel > a), ZS - rel, 0), axis=0, keepdims=True)
        odd = lax.rem(lane[:1], 2)
        cost = (p + m) * 16 + jnp.where(odd == 0, a, ZS - 1 - a)
        if a == 0:
            best, plus, minus = cost, p, m
        else:
            better = cost < best
            best, plus, minus = (
                jnp.where(better, cost, best), jnp.where(better, p, plus), jnp.where(better, m, minus)
            )
    remain = [plus - rel, minus - back]
    never = jnp.int32(1 << 20)
    todo = [jnp.where(w > 0, 1, 0) for w in remain]
    ready = [jnp.where(rel == 0, 0, never)] * 2
    key = [w * NBLK + lane for w in remain]
    shift = (1, ZS - 1)

    def rnd(r, c):
        out = []
        for way in range(2):
            todo_, ready_, sent_, block_ = c[way]
            cand = (todo_ > 0) & (ready_ <= r)
            k = jnp.where(cand, key[way], -1)
            top = jnp.max(k, axis=1, keepdims=True)
            one = jnp.where(cand & (k == top), 1, 0)
            block_ = jnp.where((lane == r) & (top >= 0), lax.rem(jnp.maximum(top, 0), NBLK), block_)
            sent_ = jnp.where(one > 0, r, sent_)
            ready_ = jnp.where(pltpu.roll(one, shift[way], 0) > 0, r + LAG, ready_)
            out.append((todo_ - one, ready_, sent_, block_))
        return tuple(out)

    zero = jnp.zeros((ZS, NBLK), jnp.int32)
    init = tuple((todo[w], ready[w], zero + ROUNDS, zero) for w in range(2))
    done = lax.fori_loop(0, ROUNDS, rnd, init)
    slots, came = [], []
    for way in range(2):
        todo_, _, sent_, block_ = done[way]
        arrival = pltpu.roll(sent_, shift[way], 0)
        slots.append(
            jnp.where(rel == 0, own, PLANE + way * ROUNDS + jnp.minimum(arrival, ROUNDS - 1))
        )
        came.append(arrival < ROUNDS)
        tab[pl.ds((T_BLOCK + way) * ZS, ZS), :] = block_
        tab[pl.ds((T_ROUND + way) * ZS, ZS), :] = sent_
        tab[pl.ds((T_SLOT + way) * ZS, ZS), :] = slots[way]
    tab[pl.ds(T_PICK * ZS, ZS), :] = jnp.where(came[0], slots[0], slots[1])
    tab[pl.ds(T_LAST * ZS, ZS), :] = last
    need = jnp.maximum(*[
        jnp.where(done[w][0] > 0, ROUNDS + 1, jnp.where(remain[w] > 0, done[w][2] + 1, 0))
        for w in range(2)
    ])
    tab[pl.ds(T_NEED * ZS, ZS), :] = jnp.broadcast_to(
        jnp.max(jnp.max(need, axis=1, keepdims=True), axis=0, keepdims=True), (ZS, NBLK)
    )


R_P0, R_P3, R_B0, R_HM, R_BE, R_GB, R_ST = 0, 4, 8, 12, 16, 18, 20
R_ALL = 24


def routed(
    rounds, idx, tab, gain, q_hbm, k_hbm, v_hbm, g_hbm,
    n_out, dq_out, dk_out, dv_out,
    qv, kx, vx, gv, rk, rv, pst, att, sq, sc, st, hs, ga,
    dks, dvs, kacc, vacc, kbs, vbs, kbr, vbr, hk, hv, nv,
    buf0, buf1, buf2, buf3, lf0, lf1, lf2, lf3, lb0, lb1, lb2, lb3,
    p0, p1, p2, p3, t0, t1, t2, t3, u0, u1, stage0, stage1, prevs,
    ssem, rsem, lsem, osem, zfs, zbs, zss,
):
    cx = lax.axis_index("ctx")
    hd = lax.axis_index("head")
    x, z = cx // ZS, lax.rem(cx, ZS)
    nxt = lax.rem(cx + 1, CTX)
    prv = lax.rem(cx + CTX - 1, CTX)
    up = lax.rem(z + ZS - 1, ZS)
    down = lax.rem(z + 1, ZS)
    ring = (x * ZS + down, x * ZS + up)
    sender = (up, down)
    buf, lf, lb = (buf0, buf1, buf2, buf3), (lf0, lf1, lf2, lf3), (lb0, lb1, lb2, lb3)
    pp, tt, u, stage = (p0, p1, p2, p3), (t0, t1, t2, t3), (u0, u1), (stage0, stage1)

    loads = [
        pltpu.make_async_copy(q_hbm, qv, lsem.at[0]),
        pltpu.make_async_copy(k_hbm, kx.at[pl.ds(1, NB)], lsem.at[1]),
        pltpu.make_async_copy(v_hbm, vx.at[pl.ds(1, NB)], lsem.at[2]),
        pltpu.make_async_copy(g_hbm, gv, lsem.at[3]),
    ]
    for c in loads:
        c.start()

    def xpeer(d):
        return lax.rem(x + d, XS)

    bar = pltpu.get_barrier_semaphore()
    for d in range(1, XS):
        pl.semaphore_signal(bar, 1, device_id=(xpeer(d) * ZS + z, hd), device_id_type=MESH)
    for t in (*ring, nxt, prv):
        pl.semaphore_signal(bar, 1, device_id=(t, hd), device_id_type=MESH)

    def greet_head(d, _):
        pl.semaphore_signal(bar, 1, device_id=(cx, lax.rem(hd + d, PEERS)), device_id_type=MESH)
        return 0

    lax.fori_loop(1, PEERS, greet_head, 0)
    pl.semaphore_wait(bar, XS - 1 + 4 + PEERS - 1)

    def remote(src, dst, send, recv, target):
        pltpu.make_async_remote_copy(
            src, dst, send, recv, device_id=target, device_id_type=MESH
        ).start()

    def spread(src_of, dst, s):
        for d in (1, 3, 2):
            t = xpeer(d)
            remote(src_of(t), dst, ssem.at[s], rsem.at[s], (t * ZS + z, hd))
        pltpu.make_async_copy(src_of(x), dst, rsem.at[s]).start()

    def arrived(ref, s):
        pltpu.make_async_copy(ref, ref, rsem.at[s]).wait()

    def sent(ref, s):
        pltpu.make_async_copy(ref, ref, ssem.at[s]).wait()

    def quarter(t):
        return pl.ds(pl.multiple_of(t * QROWS, QROWS), QROWS)

    def chunk_cols(c):
        return pl.ds(CHUNKS[c][0] * HDIM, CHUNKS[c][1] * HDIM)

    def mine(t):
        return pl.ds(t * NB, NB)

    def quarters_out(i):
        src, cols = (k_hbm, k_hbm, v_hbm, v_hbm)[i], chunk_cols(i % 2)
        spread(lambda t: src.at[:, quarter(t), cols], buf[i].at[mine(x)], R_P0 + i)

    quarters_out(0)
    quarters_out(1)
    remote(k_hbm.at[NB - 1], kx.at[0], ssem.at[R_BE], rsem.at[R_BE], (nxt, hd))
    remote(v_hbm.at[NB - 1], vx.at[0], ssem.at[R_BE + 1], rsem.at[R_BE + 1], (nxt, hd))

    def request(l):
        return idx[l // NB * (NB * ZS) + z * NB + lax.rem(l, NB)]

    def find(l, _):
        want = request(l)

        def look(m, found):
            return jnp.where(request(m) == want, m, found)

        prevs[l] = lax.fori_loop(0, l, look, PLANE)
        return 0

    lax.fori_loop(0, PLANE, find, 0)

    def slot_wait(c, way, t):
        ref = stage[c].at[way, lax.rem(t, 4)]
        pltpu.make_async_copy(ref, ref, zss.at[(c * 2 + way) * 4 + lax.rem(t, 4)]).wait()

    def drain_sends():
        for c in range(2):
            for way in range(2):
                for t in range(rounds - 4, rounds):
                    slot_wait(c, way, t)

    def landed(ref, sem):
        pltpu.make_async_copy(ref, ref, sem).wait()

    def take_forward(i, way, r):
        n = way * ROUNDS + r
        landed(lf[i].at[n], zfs.at[i * 2 * ROUNDS + n])
        buf[i][PLANE + n] = lf[i][n]

    def ring_forward(arr, between):
        def rnd(r, _):
            for c in range(2):
                i = arr * 2 + c
                for way in range(2):

                    @pl.when(r >= LAG)
                    def _():
                        take_forward(i, way, r - LAG)

                    @pl.when(r >= 4)
                    def _():
                        slot_wait(c, way, r)

                    j = tab[(T_BLOCK + way) * ZS + z, r]
                    n = way * ROUNDS + r
                    stage[c][way, lax.rem(r, 4)] = buf[i][tab[(T_SLOT + way) * ZS + z, j]]
                    remote(
                        stage[c].at[way, lax.rem(r, 4)],
                        lf[i].at[n],
                        zss.at[(c * 2 + way) * 4 + lax.rem(r, 4)],
                        zfs.at[i * 2 * ROUNDS + n],
                        (ring[way], hd),
                    )
            between(r)
            return 0

        lax.fori_loop(0, rounds, rnd, 0)
        for r in range(rounds - LAG, rounds):
            for c in range(2):
                for way in range(2):
                    take_forward(arr * 2 + c, way, r)
        drain_sends()

    def hand_out(i):
        def one(l, _):
            pp[i][l] = buf[i][tab[T_PICK * ZS + z, request(l)]]
            return 0

        lax.fori_loop(0, PLANE, one, 0)
        dst = (rk, rk, rv, rv)[i]
        spread(
            lambda t: pp[i].at[mine(t)], dst.at[:, quarter(x), chunk_cols(i % 2)], R_P3 + i
        )

    def handed(i):
        ref = (rk, rk, rv, rv)[i]
        arrived(ref.at[:, :, chunk_cols(i % 2)], R_P3 + i)

    causal = lax.broadcasted_iota(jnp.int32, (BLOCK, BLOCK), 0) <= lax.broadcasted_iota(
        jnp.int32, (BLOCK, BLOCK), 1
    )

    def head_cols(h):
        return pl.ds(pl.multiple_of(h * HDIM, HDIM), HDIM)

    def softmax_item(b, h):
        cols = head_cols(h)
        q = qv[b, :, cols]
        s0 = jnp.where(causal, dot(kx[b + 1, :, cols], q, NT), -jnp.inf)
        s1 = jnp.where(cx * NB + b > 0, dot(kx[b, :, cols], q, NT), -jnp.inf)
        s2 = dot(rk[b, :, cols], q, NT)
        m = jnp.max(jnp.maximum(jnp.maximum(s0, s1), s2), axis=0, keepdims=True)
        e = [jnp.exp2((s - m) * (SCALE * LOG2E)) for s in (s0, s1, s2)]
        r = 1.0 / jnp.sum(e[0] + e[1] + e[2], axis=0, keepdims=True)
        p = [(w * r).astype(jnp.bfloat16) for w in e]
        for n in range(3):
            pst[b, h, n] = p[n]
        att[b, :, cols] = dot(p[0], vx[b + 1, :, cols], TN) + dot(p[1], vx[b, :, cols], TN)

    def attend_item(b, h):
        cols = head_cols(h)
        o = att[b, :, cols] + dot(pst[b, h, 2], rv[b, :, cols], TN)
        att[b, :, cols] = o
        lifted = gain[:, cols] * gv[b, :, cols].astype(jnp.float32)
        sq[b] += o * o
        sc[b] += lifted * o

    def items(run):
        def between(r):
            @pl.when(r < NB * HEADS // 2)
            def _():
                for e in range(2):
                    n = r * 2 + e
                    run(n // HEADS, lax.rem(n, HEADS))

        return between

    def idle(r):
        pass

    for i in (0, 1):
        arrived(buf[i].at[pl.ds(0, PLANE)], R_P0 + i)
    quarters_out(2)
    quarters_out(3)
    ring_forward(0, idle)
    hand_out(0)
    hand_out(1)
    for i in (2, 3):
        arrived(buf[i].at[pl.ds(0, PLANE)], R_P0 + i)

    ring_forward(1, idle)
    hand_out(2)
    hand_out(3)
    for c in loads:
        c.wait()
    arrived(kx.at[0], R_BE)
    arrived(vx.at[0], R_BE + 1)
    sq[...] = jnp.zeros_like(sq)
    sc[...] = jnp.zeros_like(sc)
    for i in (0, 1):
        handed(i)

    def soften(n, _):
        softmax_item(n // HEADS, lax.rem(n, HEADS))
        return 0

    lax.fori_loop(0, NB * HEADS, soften, 0)
    for i in (2, 3):
        handed(i)

    def stats(b, _):
        def attend(h, _):
            attend_item(b, h)
            return 0

        lax.fori_loop(0, HEADS, attend, 0)
        st[b] = jnp.zeros((8, BLOCK), jnp.float32)
        st[b, 0:1, :] = jnp.sum(jnp.transpose(sq[b]), axis=0, keepdims=True)
        st[b, 1:2, :] = jnp.sum(jnp.transpose(sc[b]), axis=0, keepdims=True)

        def one(d, _):
            s = R_ST + b
            remote(
                st.at[b], hs.at[b, hd], ssem.at[s], rsem.at[s], (cx, lax.rem(hd + d, PEERS))
            )
            return 0

        lax.fori_loop(1, PEERS, one, 0)
        pltpu.make_async_copy(st.at[b], hs.at[b, hd], rsem.at[R_ST + b]).start()
        return 0

    lax.fori_loop(0, NB, stats, 0)

    def gather_terms(arr, b):
        src = (dks, dvs)[arr]
        for c in range(2):
            i = arr * 2 + c
            spread(
                lambda t: src.at[b, quarter(t), chunk_cols(c)],
                tt[i].at[x * NB + b],
                R_B0 + i,
            )

    def norm(b, _):
        arrived(hs.at[b], R_ST + b)
        total = jnp.sum(hs[b], axis=0)
        inv_row = lax.rsqrt(total[0:1, :] / WIDTH + EPS)
        cen_row = inv_row * inv_row * inv_row * total[1:2, :] / WIDTH
        inv = jnp.transpose(jnp.broadcast_to(inv_row, (HDIM, BLOCK)))
        cen = jnp.transpose(jnp.broadcast_to(cen_row, (HDIM, BLOCK)))

        def one(h, _):
            cols = head_cols(h)
            a = att[b, :, cols]
            w = gain[:, cols]
            nv[b, :, cols] = (a * inv * w).astype(jnp.bfloat16)
            lifted = w * gv[b, :, cols].astype(jnp.float32)
            d = (inv * lifted - a * cen).astype(jnp.bfloat16)
            ga[b, :, cols] = d
            dvs[b, :, cols] = dot(pst[b, h, 2], d, NN).astype(jnp.bfloat16)
            return 0

        lax.fori_loop(0, HEADS, one, 0)
        pltpu.make_async_copy(nv.at[b], n_out.at[b], osem.at[0]).start()
        gather_terms(1, b)
        return 0

    lax.fori_loop(0, NB, norm, 0)


    def backward_item(b, h):
        cols = head_cols(h)
        q = qv[b, :, cols]
        d = ga[b, :, cols]
        ks = (kx[b + 1, :, cols], kx[b, :, cols], rk[b, :, cols])
        vs = (vx[b + 1, :, cols], vx[b, :, cols], rv[b, :, cols])
        ps = [pst[b, h, n] for n in range(3)]
        dp = [dot(v, d, NT) for v in vs]
        pf = [p.astype(jnp.float32) for p in ps]
        row = jnp.sum(pf[0] * dp[0] + pf[1] * dp[1] + pf[2] * dp[2], axis=0, keepdims=True)
        ds = [(pf[n] * ((dp[n] - row) * SCALE)).astype(jnp.bfloat16) for n in range(3)]
        dk = [dot(s, q, NN) for s in ds]
        dq = dot(ds[0], ks[0], TN) + dot(ds[1], ks[1], TN) + dot(ds[2], ks[2], TN)
        gv[b, :, cols] = dq.astype(jnp.bfloat16)
        dks[b, :, cols] = dk[2].astype(jnp.bfloat16)
        vacc[b + 1, :, cols] = dot(ps[0], d, NN)
        kacc[b + 1, :, cols] = dk[0]
        kbe, vbe = dk[1].astype(jnp.bfloat16), dot(ps[1], d, NN).astype(jnp.bfloat16)

        @pl.when(b == 0)
        def _():
            kbs[:, cols] = kbe
            vbs[:, cols] = vbe

        @pl.when(b > 0)
        def _():
            kacc[b, :, cols] += kbe.astype(jnp.float32)
            vacc[b, :, cols] += vbe.astype(jnp.float32)

        @pl.when(h == HEADS - 1)
        def _():
            gather_terms(0, b)

    def combine(i):
        arrived(tt[i], R_B0 + i)
        u_ = u[i % 2]
        u_[PLANE] = jnp.zeros(u_.shape[1:], jnp.float32)

        def one(l, _):
            u_[l] = tt[i][l].astype(jnp.float32) + u_[prevs[l]]
            return 0

        lax.fori_loop(0, PLANE, one, 0)

    def ring_backward(arr, between):
        for c in range(2):
            for way in range(2):
                n = way * (ROUNDS + 1) + ROUNDS
                buf[arr * 2 + c][n] = jnp.zeros(buf[c].shape[1:], jnp.bfloat16)

        def take(i, way, r):
            n = way * ROUNDS + r
            landed(lb[i].at[n], zbs.at[i * 2 * ROUNDS + n])
            buf[i][way * (ROUNDS + 1) + r] = lb[i][n]

        def rnd(t, _):
            r = rounds - 1 - t
            for c in range(2):
                i = arr * 2 + c
                for way in range(2):

                    @pl.when(t >= LAG)
                    def _():
                        take(i, way, r + LAG)

                    @pl.when(t >= 4)
                    def _():
                        slot_wait(c, way, t)

                    j = tab[(T_BLOCK + way) * ZS + sender[way], r]
                    on = tab[(T_ROUND + way) * ZS + z, j] + way * (ROUNDS + 1)
                    n = way * ROUNDS + r
                    stage[c][way, lax.rem(t, 4)] = (
                        u[c][tab[T_LAST * ZS + z, j]] + buf[i][on].astype(jnp.float32)
                    ).astype(jnp.bfloat16)
                    remote(
                        stage[c].at[way, lax.rem(t, 4)],
                        lb[i].at[n],
                        zss.at[(c * 2 + way) * 4 + lax.rem(t, 4)],
                        zbs.at[i * 2 * ROUNDS + n],
                        (ring[1 - way], hd),
                    )
            between(t)
            return 0

        lax.fori_loop(0, rounds, rnd, 0)
        for r in range(LAG - 1, -1, -1):
            for c in range(2):
                for way in range(2):
                    take(arr * 2 + c, way, r)
        drain_sends()

    def send_home(i):
        u_, b_ = u[i % 2], buf[i]
        sent(pp[i].at[pl.ds(0, PLANE - NB)], R_P3 + i)

        def one(l, _):
            j = l // NB * (NB * ZS) + z * NB + lax.rem(l, NB)
            s = u_[tab[T_LAST * ZS + z, j]]
            s += b_[tab[T_ROUND * ZS + z, j]].astype(jnp.float32)
            s += b_[ROUNDS + 1 + tab[(T_ROUND + 1) * ZS + z, j]].astype(jnp.float32)
            pp[i][l] = s.astype(jnp.bfloat16)
            return 0

        lax.fori_loop(0, PLANE, one, 0)
        dst = (hk, hk, hv, hv)[i]
        spread(
            lambda t: pp[i].at[mine(t)], dst.at[:, quarter(x), chunk_cols(i % 2)], R_HM + i
        )

    combine(2)
    combine(3)
    ring_backward(1, items(backward_item))
    send_home(2)
    send_home(3)
    pltpu.make_async_copy(gv, dq_out, osem.at[1]).start()
    combine(0)
    combine(1)
    ring_backward(0, idle)
    remote(vbs, vbr, ssem.at[R_GB + 1], rsem.at[R_GB + 1], (prv, hd))
    remote(kbs, kbr, ssem.at[R_GB], rsem.at[R_GB], (prv, hd))
    send_home(0)
    send_home(1)

    def finish(acc, h, edge, out, dst, sem):
        def add(j, _):
            cols = head_cols(j)
            acc[NB, :, cols] += edge[:, cols].astype(jnp.float32)
            return 0

        lax.fori_loop(0, HEADS, add, 0)

        def block(b, _):
            def head(j, _):
                cols = head_cols(j)
                out[b, :, cols] = (
                    acc[b + 1, :, cols] + h[b, :, cols].astype(jnp.float32)
                ).astype(jnp.bfloat16)
                return 0

            lax.fori_loop(0, HEADS, head, 0)
            pltpu.make_async_copy(out.at[b], dst.at[b], osem.at[sem]).start()
            return 0

        lax.fori_loop(0, NB, block, 0)

    def terms_sent(i):
        src = (dks, dks, dvs, dvs)[i]
        sent(src.at[:, pl.ds(0, BLOCK - QROWS), chunk_cols(i % 2)], R_B0 + i)

    for i in (2, 3):
        terms_sent(i)
        arrived(hv.at[:, :, chunk_cols(i % 2)], R_HM + i)
    arrived(vbr, R_GB + 1)
    finish(vacc, hv, vbr, dvs, dv_out, 2)
    for i in (0, 1):
        terms_sent(i)
        arrived(hk.at[:, :, chunk_cols(i % 2)], R_HM + i)
    arrived(kbr, R_GB)
    finish(kacc, hk, kbr, dks, dk_out, 3)

    for i in range(4):
        sent(buf[i].at[pl.ds(0, PLANE - NB)], R_P0 + i)
        sent(pp[i].at[pl.ds(0, PLANE - NB)], R_HM + i)
    for s in (R_BE, R_BE + 1, R_GB, R_GB + 1):
        sent(kbs, s)
    for b in range(NB):
        sent(hs.at[b, pl.ds(0, PEERS - 1)], R_ST + b)
    for s, (src, dst) in enumerate(((nv, n_out), (gv, dq_out), (dvs, dv_out), (dks, dk_out))):
        pltpu.make_async_copy(src, dst, osem.at[s]).wait()


def by_route(level, table, gain, q, k, v, g, sort_index):
    bf, f32 = jnp.bfloat16, jnp.float32
    blocks = (NB, BLOCK, COLS)
    vm, dma = pltpu.VMEM, pltpu.SemaphoreType.DMA
    full, one = vm(blocks, bf), vm((BLOCK, COLS), bf)
    more = (NB + 1, BLOCK, COLS)
    widths = [n * HDIM for _, n in CHUNKS]

    def per_pass(n):
        return [vm((n, QROWS, widths[i % 2]), bf) for i in range(4)]

    scratch = [
        full, vm(more, bf), vm(more, bf), full, full, full,
        vm((NB, HEADS, 3, BLOCK, BLOCK), bf), vm(blocks, f32),
        vm((NB, BLOCK, HDIM), f32), vm((NB, BLOCK, HDIM), f32),
        vm((NB, 8, BLOCK), f32), vm((NB, PEERS, 8, BLOCK), f32), full,
        full, full, vm(more, f32), vm(more, f32),
        one, one, one, one, full, full, full,
        *per_pass(PLANE + 2 * ROUNDS), *per_pass(2 * ROUNDS), *per_pass(2 * ROUNDS),
        *per_pass(PLANE), *per_pass(PLANE),
        *[vm((PLANE + 1, QROWS, w), f32) for w in widths],
        *[vm((2, 4, QROWS, w), bf) for w in widths],
        pltpu.SMEM((PLANE,), jnp.int32),
        dma((R_ALL,)), dma((R_ALL,)), dma((4,)), dma((4,)),
        dma((8 * ROUNDS,)), dma((8 * ROUNDS,)), dma((16,)),
    ]
    smem = pl.BlockSpec(memory_space=pltpu.SMEM)
    anywhere = pl.BlockSpec(memory_space=pl.ANY)
    return tuple(
        pl.pallas_call(
            functools.partial(routed, LEVELS[level]),
            out_shape=[jax.ShapeDtypeStruct(blocks, bf)] * 4,
            in_specs=[smem, smem, pl.BlockSpec(memory_space=pltpu.VMEM)] + [anywhere] * 4,
            out_specs=[anywhere] * 4,
            scratch_shapes=scratch,
            compiler_params=pltpu.CompilerParams(
                collective_id=1 + level, has_side_effects=True, vmem_limit_bytes=62 << 20
            ),
        )(sort_index, table, gain, q, k, v, g)
    )


def by_shares(table, gain, q, k, v, g, sort_index):
    bf, f32 = jnp.bfloat16, jnp.float32
    blocks = (NB, BLOCK, COLS)
    vm = pltpu.VMEM
    slices = vm((NBLK, ROWS, COLS), bf)
    full = vm(blocks, bf)
    one = vm((BLOCK, COLS), bf)
    scratch = [
        full, vm((NB + 1, BLOCK, COLS), bf), vm((NB + 1, BLOCK, COLS), bf), full,
        slices, slices, slices, slices, full, full,
        vm((2, HEADS, 3, BLOCK, BLOCK), bf), vm((2, BLOCK, COLS), f32),
        vm((BLOCK, HDIM), f32), vm((BLOCK, HDIM), f32),
        vm((NB, 8, BLOCK), f32), vm((NB, PEERS, 8, BLOCK), f32), one,
        full, full, vm((NB + 1, BLOCK, COLS), f32), vm((NB + 1, BLOCK, COLS), f32),
        one, one, one, one, slices, slices, full, full,
        vm((1, NBLK * ROWS), jnp.int32), full, full,
        pltpu.SemaphoreType.DMA((NSEM,)), pltpu.SemaphoreType.DMA((NSEM,)),
        pltpu.SemaphoreType.DMA((4,)), pltpu.SemaphoreType.DMA((4,)),
    ]
    anywhere = pl.BlockSpec(memory_space=pl.ANY)
    return tuple(
        pl.pallas_call(
            kernel,
            out_shape=[jax.ShapeDtypeStruct(blocks, bf)] * 4,
            in_specs=[
                pl.BlockSpec(memory_space=pltpu.SMEM),
                pl.BlockSpec(memory_space=pltpu.VMEM),
                anywhere, anywhere, anywhere, anywhere,
            ],
            out_specs=[anywhere] * 4,
            scratch_shapes=scratch,
            compiler_params=pltpu.CompilerParams(
                collective_id=0, has_side_effects=True, vmem_limit_bytes=60 << 20
            ),
        )(sort_index, gain, q, k, v, g)
    )


def on_device(queries, key_rows, value_rows, norm_gain, sort_index, grad_normed):
    blocks = (NB, BLOCK, COLS)
    table = pl.pallas_call(
        router,
        out_shape=jax.ShapeDtypeStruct(((T_NEED + 1) * ZS, NBLK), jnp.int32),
        in_specs=[pl.BlockSpec(memory_space=pltpu.SMEM)],
        out_specs=pl.BlockSpec(memory_space=pltpu.VMEM),
    )(sort_index)
    need = table[T_NEED * ZS, 0]
    outs = lax.switch(
        sum(jnp.where(need > n, 1, 0) for n in LEVELS),
        [functools.partial(by_route, n) for n in range(len(LEVELS))] + [by_shares],
        table, norm_gain.reshape(1, COLS), queries.reshape(blocks), key_rows.reshape(blocks),
        value_rows.reshape(blocks), grad_normed.reshape(blocks), sort_index,
    )
    return tuple(o.reshape(NB * BLOCK, COLS) for o in outs)


def solution(mesh):
    split = P("ctx", "head")
    return jax.shard_map(
        on_device,
        mesh=mesh,
        in_specs=(split, split, split, P("head"), P(), split),
        out_specs=(split, split, split, split),
        check_vma=False,
    )
```
